256 devices in a mesh: space: 32 (over z, x_lo, core), filt: 8 (over y, x_hi).
Axes of the slice: x: 4 (x_hi: 2, x_lo: 2; x = x_hi * 2 + x_lo), y: 4, z: 8, core: 2. Of those that a mesh axis runs over, the one named last changes fastest.
Arguments:
- volume: bfloat16 [64, 128, 32, 128], P('space', 'filt'), may hold values from -6 to 6
- kernel: bfloat16 [3, 3, 3, 256, 128], P(None, None, None, 'filt'), may hold values from -0.109375 to 0.109375
- out_grad: bfloat16 [32, 64, 16, 256], P('space', None, None, 'filt'), may hold values from -6 to 6
Outputs:
- features: bfloat16 [32, 64, 16, 256], P('space', None, None, 'filt')
- in_grad: bfloat16 [64, 128, 32, 128], P('space', 'filt')
- kernel_grad: float32 [3, 3, 3, 256, 128], P(None, None, None, 'filt')
The draws below stay inside these ranges and needn't reach their ends.
All inputs are finite; a program needn't handle non-finite values.
Results may differ from the reference program's by a relative error of at most 0.001.
Values may be sent and summed in bfloat16 or wider, within the bound.
A program may use at most 64 MiB of HBM per device.

```python
import jax
import jax.numpy as jnp
from jax import lax

CIN = 128
COUT = 256
NZ = 32
NX = 64
NY = 128


def steps_of(own_key, extent, shards, smallest, largest):
    level, own = 1.0, jax.random.fold_in(own_key, 6)
    for position, blocks in shards:
        steps = jnp.exp(jax.random.uniform(jax.random.fold_in(own, position), (blocks,), jnp.float32, smallest / len(shards), largest / len(shards)))
        level = level * jnp.repeat(steps, extent[position] // blocks).reshape([-1 if axis == position else 1 for axis in range(len(extent))])
    return level


def gaussian(own_key, extent, scale, bound, shards=(), held_as=jnp.bfloat16):
    level = steps_of(own_key, extent, shards, -0.22, 0.18) if shards else 1.0
    entries = jax.random.normal(own_key, extent, jnp.float32) * scale * level
    return jnp.minimum(jnp.maximum(entries, -bound), bound).astype(held_as)


def setup_inputs(seed: int = 0) -> dict:
    splits = jax.random.split(jax.random.key(seed), 4)
    volume = gaussian(splits[0], (NX, NY, NZ, CIN), 1.0, 6.0, ((0, 32), (1, 8)))
    kernel = gaussian(splits[1], (3, 3, 3, COUT, CIN), (27 * CIN) ** -0.5, 0.109375, ((3, 8),))
    out_grad = gaussian(splits[2], (NX // 2, NY // 2, NZ // 2, COUT), 1.0, 6.0, ((0, 32), (3, 8)))
    return dict(volume=volume, kernel=kernel, out_grad=out_grad)


def take_patch(padded, a, b, c, dims):
    ox, oy, oz = dims
    chan = padded.shape[3]
    return lax.slice(padded, (a, b, c, 0), (a + 2 * ox - 1, b + 2 * oy - 1, c + 2 * oz - 1, chan), (2, 2, 2, 1))


def reference(volume, kernel, out_grad):
    ox, oy, oz, cout = out_grad.shape
    cin = volume.shape[3]
    dims = (ox, oy, oz)
    padded = jnp.pad(volume, ((1, 1), (1, 1), (1, 1), (0, 0)))
    grad_rows = out_grad.reshape(-1, cout)
    total = jnp.zeros((ox * oy * oz, cout), jnp.float32)
    scatter = jnp.zeros((volume.shape[0] + 2, volume.shape[1] + 2, volume.shape[2] + 2, cin), jnp.float32)
    pieces = []
    for a in range(3):
        for b in range(3):
            for c in range(3):
                patch = take_patch(padded, a, b, c, dims).reshape(-1, cin)
                total = total + lax.dot_general(patch, kernel[a, b, c], (((1,), (1,)), ((), ())), preferred_element_type=jnp.float32)
                pieces.append(lax.dot_general(grad_rows, patch, (((0,), (0,)), ((), ())), preferred_element_type=jnp.float32))
                contrib = jnp.dot(grad_rows, kernel[a, b, c], preferred_element_type=jnp.float32)
                scatter = scatter.at[a:a + 2 * ox - 1:2, b:b + 2 * oy - 1:2, c:c + 2 * oz - 1:2].add(contrib.reshape(ox, oy, oz, cin))
    features = total.reshape(ox, oy, oz, cout).astype(jnp.bfloat16)
    in_grad = scatter[1:-1, 1:-1, 1:-1].astype(jnp.bfloat16)
    factor = float(ox * oy * oz) ** -0.5
    kernel_grad = jnp.stack(pieces).reshape(3, 3, 3, cout, cin) * factor
    return features, in_grad, kernel_grad
```

```python
import jax
import jax.numpy as jnp
from jax import lax
from jax.experimental import pallas as pl
from jax.experimental.pallas import tpu as pltpu
from jax.sharding import PartitionSpec as P

MESH = pl.DeviceIdType.MESH
F32 = jnp.float32
BF16 = jnp.bfloat16
NF = 8
NS = 32
NQ = 16
KS = [2 * t + e for e in range(2) for t in range(8)]

TAPS = {}
for _p in range(8):
    _x, _y, _z = _p // 4, (_p // 2) % 2, _p % 2
    TAPS[(0, _p)] = (1 + _x, 1 + _y, 1 + _z)
    if _z:
        TAPS[(1, _p)] = (1 + _x, 1 + _y, 0)
    if _x:
        TAPS[(2, _p)] = (0, 1 + _y, 1 + _z)
    if _y:
        TAPS[(3, _p)] = (1 + _x, 0, 1 + _z)
TAPS[(1, 4)] = (0, 1, 0)
TAPS[(1, 6)] = (0, 2, 0)
TAPS[(1, 0)] = (0, 0, 0)
TAPS[(2, 0)] = (0, 0, 1)
TAPS[(2, 1)] = (0, 0, 2)
TAPS[(3, 4)] = (1, 0, 0)
TAPS[(3, 0)] = (2, 0, 0)


def swap_blocks(arrs, unit):
    lane = lax.broadcasted_iota(jnp.int32, arrs[0].shape, 1)
    arrs = list(arrs)
    for bit in (4, 2, 1):
        step = bit * unit
        low = (lane & step) == 0
        for i in range(8):
            if i & bit:
                continue
            lo, hi = arrs[i], arrs[i | bit]
            arrs[i] = jnp.where(low, lo, pltpu.roll(hi, step, 1))
            arrs[i | bit] = jnp.where(low, pltpu.roll(lo, 128 - step, 1), hi)
    return arrs


def lane_blocks(shape, blocks):
    blk = lax.broadcasted_iota(jnp.int32, shape, 1) >> 4
    hit = blk == blocks[0]
    for b in blocks[1:]:
        hit = hit | (blk == b)
    return hit


def shift_row(w):
    row = lax.broadcasted_iota(jnp.int32, w.shape, 0)
    first = (row & 7) == 0
    prev = jnp.where(row < 128, 0.0, pltpu.roll(w, 121, 0))
    return jnp.where(first, prev, pltpu.roll(w, 1, 0))


def shift_depth(w):
    w = w.reshape(8, 16, 8, 128)
    even, odd = w[:, :8], w[:, 8:]
    back = jnp.concatenate([jnp.zeros_like(odd[:, :1]), odd[:, :7]], axis=1)
    return jnp.concatenate([back, even], axis=1).reshape(1024, 128)


def four_shifts(w_bf16):
    w = w_bf16.astype(F32).reshape(1024, 128)
    wj = shift_row(w)
    return [w.astype(BF16), shift_depth(w).astype(BF16), wj.astype(BF16), shift_depth(wj).astype(BF16)]


def selection(dj, dk):
    m = lax.broadcasted_iota(jnp.int32, (128, 256), 0)
    n = lax.broadcasted_iota(jnp.int32, (128, 256), 1)
    row = (m & 7) + dj
    k = 2 * ((m >> 3) & 7) + (m >> 6) + dk
    lane = (row >> 3) * 128 + (k & 1) * 64 + (k >> 1) * 8 + (row & 7)
    return jnp.where((n == lane) & (k < 16), 1.0, 0.0).astype(BF16)


def dot_t(x, y):
    return lax.dot_general(x, y, (((1,), (1,)), ((), ())), preferred_element_type=F32)


def body(
    vol, ker, grad, feat_out, ig_out, kg_out,
    vf, halo_b, halo_r, halo_c, vs, wbuf, gs, gtb, gnext, kall, rhs, rt, s1, asum, s2, own3, kb, fs, fb, pb, gv, igf,
    snd_g, rcv_g, snd_v, rcv_v, snd_k, rcv_k, snd_h, rcv_h, snd_m, rcv_m, snd_2, rcv_2, snd_3, rcv_3, snd_f, rcv_f,
):
    s = lax.axis_index("space")
    f = lax.axis_index("filt")
    core = s % 2
    q = s // 2
    sib = s + 1 - 2 * core
    sx = s + 2 - 4 * (q % 2)
    up = (s + 1) % NS
    down = (s + NS - 1) % NS
    fup = (f + 1) % NF
    fdown = (f + NF - 1) % NF
    fx = f + 1 - 2 * (f % 2)
    dest = q // 2
    half = q % 2

    barrier = pltpu.get_barrier_semaphore()
    hello = [(s, (f + i) % NF) for i in range(1, NF)]
    hello += [(sx, (fx + 2 * i) % NF) for i in range(4)]
    hello += [(sib, f), (down, f), (up, f), (down, fdown)]
    hello += [(2 * ((q + i) % NQ) + core, f) for i in range(1, NQ)]
    hello += [(2 * (2 * f + r) + core, (f + i) % NF) for r in range(2) for i in range(NF)]
    for dev in hello:
        pl.semaphore_signal(barrier, inc=1, device_id=dev, device_id_type=MESH)

    sent = []

    def copy(src, dst, ss, rs, dev):
        c = pltpu.make_async_remote_copy(
            src_ref=src, dst_ref=dst, send_sem=ss, recv_sem=rs, device_id=dev, device_id_type=MESH
        )
        return c

    def send(*args):
        c = copy(*args)
        c.start()
        sent.append(c)

    def arrived(dst, ss, rs):
        copy(dst, dst, ss, rs, (sib, f)).wait_recv()

    for px in range(2):
        vf[pl.ds(((1 + px) * 17 + 1) * 32, 512), :] = vol[px].astype(F32).reshape(512, 128)
    parity = []
    for p in range(8):
        a, b, z = 1 + p // 4, 1 + (p // 2) % 2, p % 2
        parity.append(
            jnp.concatenate([vf[pl.ds((a * 17 + b) * 32 + 2 * k + z, 8, stride=64), :] for k in KS], axis=0)
        )
    for i, x in enumerate(swap_blocks(parity, 16)):
        vs[i] = x.astype(BF16)
    tiles = [
        jnp.concatenate([grad[2 * t].astype(F32), grad[2 * t + 1].astype(F32)], axis=1) for t in range(8)
    ]
    for i, x in enumerate(swap_blocks(tiles, 8)):
        gs[i] = x.astype(BF16)

    pl.semaphore_wait(barrier, len(hello))

    for i in range(1, NF):
        to = (f + i) % NF
        send(gs, gtb.at[:, f], snd_g.at[i - 1], rcv_g.at[i - 1], (s, to))
    for i in range(1, NF):
        to = (f + i) % NF
        send(vs.at[to], wbuf.at[0, f], snd_v.at[i - 1], rcv_v.at[i - 1], (s, to))
    for i in range(1, 4):
        send(ker.at[:, core], kall.at[:, f, core], snd_k.at[i - 1], rcv_k.at[i - 1], (s, (f + 2 * i) % NF))
    for i in range(4):
        send(ker.at[:, core], kall.at[:, f, core], snd_k.at[3 + i], rcv_k.at[3 + i], (sx, (fx + 2 * i) % NF))
    send(vol.at[1], halo_b, snd_h.at[0], rcv_h.at[0], (up, f))
    send(vol.at[:, 15], halo_r, snd_h.at[1], rcv_h.at[1], (s, fup))
    send(vol.at[1, 15], halo_c, snd_h.at[2], rcv_h.at[2], (up, fup))

    wbuf[0, f] = vs[f]
    gtb[:, f] = gs[...]
    kall[:, f, core] = ker[:, core]

    for i in range(1, NF):
        arrived(wbuf.at[0, (f + NF - i) % NF], snd_v.at[i - 1], rcv_v.at[i - 1])
    send(wbuf.at[0], wbuf.at[1], snd_m.at[0], rcv_m.at[0], (up, f))
    for i, x in enumerate(four_shifts(wbuf[0])):
        rhs[:, i * 128 : i * 128 + 128] = x
    for i in range(1, NF):
        arrived(gtb.at[:, (f + NF - i) % NF], snd_g.at[i - 1], rcv_g.at[i - 1])
    send(gtb.at[f], gnext.at[0], snd_m.at[1], rcv_m.at[1], (down, f))
    send(gtb.at[fup], gnext.at[1], snd_m.at[2], rcv_m.at[2], (down, f))
    gall = jnp.concatenate([gtb[t].reshape(256, 128) for t in range(8)], axis=1)
    own = jnp.dot(gall, rhs[...], preferred_element_type=F32)

    arrived(wbuf.at[1], snd_m.at[0], rcv_m.at[0])
    for i, x in enumerate(four_shifts(wbuf[1])):
        rhs[:, i * 128 : i * 128 + 128] = jnp.where(s > 0, x, jnp.zeros_like(x))
    below = jnp.dot(gall, rhs[...], preferred_element_type=F32)
    o = [own[:, i * 128 : i * 128 + 128] for i in range(4)]
    b = [below[:, i * 128 : i * 128 + 128] for i in range(4)]
    shape = (256, 128)
    rt[0] = o[0]
    x = jnp.where(lane_blocks(shape, (4, 6)), pltpu.roll(b[1], 112, 1), o[1])
    rt[1] = jnp.where(lane_blocks(shape, (0,)), pltpu.roll(b[3], 16, 1), x)
    rt[2] = jnp.where(lane_blocks(shape, (0, 1)), pltpu.roll(b[2], 32, 1), b[0])
    rt[3] = jnp.where(lane_blocks(shape, (0, 4)), pltpu.roll(o[3], 16, 1), o[2])

    send(rt.at[pl.ds(2 * (1 - core), 2)], s1, snd_m.at[3], rcv_m.at[3], (sib, f))
    for i in range(1, 4):
        arrived(kall.at[:, (f + NF - 2 * i) % NF, core], snd_k.at[i - 1], rcv_k.at[i - 1])
    for i in range(4):
        arrived(kall.at[:, (fx + NF - 2 * i) % NF, core], snd_k.at[3 + i], rcv_k.at[3 + i])
    send(kall.at[:, :, core], kall.at[:, :, core], snd_m.at[4], rcv_m.at[4], (sib, f))
    arrived(s1, snd_m.at[3], rcv_m.at[3])
    for l in range(2):
        asum[l] = (rt[2 * core + l] + s1[l]).reshape(16, 16, 128)
    for i in range(1, NQ):
        qd = (q + i) % NQ
        send(asum.at[:, qd], s2.at[i - 1], snd_2.at[i - 1], rcv_2.at[i - 1], (2 * qd + core, f))

    arrived(halo_b, snd_h.at[0], rcv_h.at[0])
    arrived(halo_r, snd_h.at[1], rcv_h.at[1])
    arrived(halo_c, snd_h.at[2], rcv_h.at[2])
    low = halo_b[...].astype(F32).reshape(512, 128)
    vf[pl.ds(32, 512), :] = jnp.where(s > 0, low, jnp.zeros_like(low))
    edge = halo_c[...].astype(F32)
    vf[pl.ds(0, 32), :] = jnp.where((s > 0) & (f > 0), edge, jnp.zeros_like(edge))
    for px in range(2):
        edge = halo_r[px].astype(F32)
        vf[pl.ds((1 + px) * 17 * 32, 32), :] = jnp.where(f > 0, edge, jnp.zeros_like(edge))
    for a in range(3):
        for b3 in range(3):
            def cells(z):
                return vf[pl.ds((a * 17 + b3) * 32 + z, 8, stride=64), :]
            for c in range(3):
                col = ((a * 3 + b3) * 3 + c) * 128
                rows = [
                    jnp.zeros((8, 128), F32) if 2 * k + c == 0 else cells(2 * k + c - 1) for k in KS
                ]
                pb[:, col : col + 128] = jnp.concatenate(rows, axis=0).astype(BF16)
    arrived(kall.at[:, :, 1 - core], snd_m.at[4], rcv_m.at[4])
    total = jnp.zeros((256, 128), F32)
    for a in range(3):
        taps = jnp.concatenate([kall[9 * a + n].reshape(256, 128) for n in range(9)], axis=1)
        total = total + dot_t(taps, pb[:, 1152 * a : 1152 * a + 1152])
    fs[...] = total.astype(BF16).reshape(8, 32, 128)
    for i in range(1, NF):
        to = (f + i) % NF
        send(fs.at[to], fb.at[f], snd_f.at[i - 1], rcv_f.at[i - 1], (s, to))
    fb[f] = fs[f]

    for i in range(1, NQ):
        arrived(s2.at[i - 1], snd_2.at[i - 1], rcv_2.at[i - 1])
    acc = asum[:, q]
    for i in range(1, NQ):
        acc = acc + s2[i - 1]
    own3[...] = acc
    slot = kb.at[f, pl.ds(2 * core, 2), half]
    for i in range(1, NQ):
        qd = (q + i) % NQ
        send(own3, slot, snd_3.at[i], rcv_3.at[8 * half + f], (2 * qd + core, dest))
    home = copy(own3, slot, snd_3.at[0], rcv_3.at[8 * half + f], (s, dest))

    @pl.when(f != dest)
    def _():
        home.start()

    @pl.when(f == dest)
    def _():
        kb[f, pl.ds(2 * core, 2), half] = own3[...]

    arrived(gnext.at[0], snd_m.at[1], rcv_m.at[1])
    arrived(gnext.at[1], snd_m.at[2], rcv_m.at[2])
    picks = jnp.concatenate([selection(dj, dk) for dj in range(2) for dk in range(2)], axis=0)
    here = gtb[f].reshape(256, 128)
    nxt = gtb[fup].reshape(256, 128)
    nxt = jnp.where(f < NF - 1, nxt, jnp.zeros_like(nxt))
    gv[0] = dot_t(picks, jnp.concatenate([here, nxt], axis=1)).astype(BF16)
    here = gnext[0].reshape(256, 128)
    here = jnp.where(s < NS - 1, here, jnp.zeros_like(here))
    nxt = gnext[1].reshape(256, 128)
    nxt = jnp.where((s < NS - 1) & (f < NF - 1), nxt, jnp.zeros_like(nxt))
    gv[1] = dot_t(picks, jnp.concatenate([here, nxt], axis=1)).astype(BF16)
    steps = (((1, 0),), ((0, 1), (2, 0)))
    for px in range(2):
        for py in range(2):
            for pz in range(2):
                left, right = [], []
                for a, di in steps[px]:
                    for b3, dj in steps[py]:
                        for c, dk in steps[pz]:
                            v = (2 * dj + dk) * 128
                            left.append(gv[di, v : v + 128])
                            right.append(kall[9 * a + 3 * b3 + c].reshape(256, 128))
                res = jnp.dot(
                    jnp.concatenate(left, axis=1), jnp.concatenate(right, axis=0), preferred_element_type=F32
                )
                for n, k in enumerate(KS):
                    igf[pl.ds((px * 16 + py) * 32 + 2 * k + pz, 8, stride=64), :] = res[8 * n : 8 * n + 8]
    ig_out[...] = igf[...].reshape(2, 16, 32, 128).astype(BF16)

    for r in range(2):
        for i in range(NF):
            src = (f + i) % NF
            got = copy(
                own3, kb.at[src, pl.ds(2 * core, 2), r], snd_3.at[0], rcv_3.at[8 * r + src], (sib, f)
            )
            if i == 0:
                @pl.when(2 * f + r != q)
                def _():
                    got.wait_recv()
            else:
                got.wait_recv()
    send(kb.at[:, pl.ds(2 * core, 2)], kb.at[:, pl.ds(2 * core, 2)], snd_m.at[5], rcv_m.at[5], (sib, f))

    for i in range(1, NF):
        arrived(fb.at[(f + NF - i) % NF], snd_f.at[i - 1], rcv_f.at[i - 1])
    for t, x in enumerate(swap_blocks([fb[i].astype(F32) for i in range(8)], 8)):
        feat_out[2 * t] = x[:, :64].astype(BF16)
        feat_out[2 * t + 1] = x[:, 64:].astype(BF16)

    arrived(kb.at[:, pl.ds(2 * (1 - core), 2)], snd_m.at[5], rcv_m.at[5])
    factor = float(32 * 64 * 16) ** -0.5
    for lt in range(4):
        blocks = swap_blocks([kb[i, lt].reshape(32, 128) for i in range(8)], 16)
        for pos in range(8):
            if (lt, pos) in TAPS:
                a, b3, c = TAPS[(lt, pos)]
                kg_out[9 * a + 3 * b3 + c] = blocks[pos] * factor

    for c in sent:
        c.wait_send()

    @pl.when(f != dest)
    def _():
        home.wait_send()


def on_device(volume, kernel, out_grad):
    vmem = pl.BlockSpec(memory_space=pltpu.VMEM)
    dma = pltpu.SemaphoreType.DMA
    feat, ig, kg = pl.pallas_call(
        body,
        out_shape=(
            jax.ShapeDtypeStruct((16, 32, 64), BF16),
            jax.ShapeDtypeStruct((2, 16, 32, 128), BF16),
            jax.ShapeDtypeStruct((27, 32, 128), F32),
        ),
        in_specs=[vmem] * 3,
        out_specs=(vmem,) * 3,
        scratch_shapes=[
            pltpu.VMEM((3 * 17 * 32, 128), F32),
            pltpu.VMEM((16, 32, 128), BF16),
            pltpu.VMEM((2, 32, 128), BF16),
            pltpu.VMEM((32, 128), BF16),
            pltpu.VMEM((8, 128, 128), BF16),
            pltpu.VMEM((2, 8, 128, 128), BF16),
            pltpu.VMEM((8, 32, 128), BF16),
            pltpu.VMEM((8, 8, 32, 128), BF16),
            pltpu.VMEM((2, 8, 32, 128), BF16),
            pltpu.VMEM((27, 8, 2, 16, 128), BF16),
            pltpu.VMEM((1024, 512), BF16),
            pltpu.VMEM((4, 256, 128), F32),
            pltpu.VMEM((2, 256, 128), F32),
            pltpu.VMEM((2, 16, 16, 128), F32),
            pltpu.VMEM((15, 2, 16, 128), F32),
            pltpu.VMEM((2, 16, 128), F32),
            pltpu.VMEM((8, 4, 2, 16, 128), F32),
            pltpu.VMEM((8, 32, 128), BF16),
            pltpu.VMEM((8, 32, 128), BF16),
            pltpu.VMEM((128, 27 * 128), BF16),
            pltpu.VMEM((2, 512, 256), BF16),
            pltpu.VMEM((2 * 16 * 32, 128), F32),
            dma((7,)), dma((7,)), dma((7,)), dma((7,)), dma((7,)), dma((7,)),
            dma((3,)), dma((3,)), dma((6,)), dma((6,)), dma((15,)), dma((15,)),
            dma((16,)), dma((16,)), dma((7,)), dma((7,)),
        ],
        compiler_params=pltpu.CompilerParams(
            collective_id=0, has_side_effects=True, vmem_limit_bytes=48 * 1024 * 1024
        ),
        name="conv_fwd_bwd",
    )(volume, kernel.reshape(27, 2, 16, 128), out_grad.transpose(0, 2, 3, 1).reshape(16, 32, 64))
    features = feat.reshape(1, 16, 32, 64).transpose(0, 3, 1, 2)
    return features, ig, kg.reshape(3, 3, 3, 32, 128)


def solution(mesh):
    return jax.shard_map(
        on_device,
        mesh=mesh,
        in_specs=(
            P("space", "filt", None, None),
            P(None, None, None, "filt", None),
            P("space", None, None, "filt"),
        ),
        out_specs=(
            P("space", None, None, "filt"),
            P("space", "filt", None, None),
            P(None, None, None, "filt", None),
        ),
        check_vma=False,
    )
```

```python
import jax
import jax.numpy as jnp
from jax import lax
from jax.experimental import pallas as pl
from jax.experimental.pallas import tpu as pltpu
from jax.sharding import PartitionSpec as P

MESH = pl.DeviceIdType.MESH
F32 = jnp.float32
BF16 = jnp.bfloat16
NF = 8
NS = 32
NQ = 16
KS = [2 * t + e for e in range(2) for t in range(8)]

TAPS = {}
for _p in range(8):
    _x, _y, _z = _p // 4, (_p // 2) % 2, _p % 2
    TAPS[(0, _p)] = (1 + _x, 1 + _y, 1 + _z)
    if _z:
        TAPS[(1, _p)] = (1 + _x, 1 + _y, 0)
    if _x:
        TAPS[(2, _p)] = (0, 1 + _y, 1 + _z)
    if _y:
        TAPS[(3, _p)] = (1 + _x, 0, 1 + _z)
TAPS[(1, 4)] = (0, 1, 0)
TAPS[(1, 6)] = (0, 2, 0)
TAPS[(1, 0)] = (0, 0, 0)
TAPS[(2, 0)] = (0, 0, 1)
TAPS[(2, 1)] = (0, 0, 2)
TAPS[(3, 4)] = (1, 0, 0)
TAPS[(3, 0)] = (2, 0, 0)


def swap_blocks(arrs, unit):
    lane = lax.broadcasted_iota(jnp.int32, arrs[0].shape, 1)
    arrs = list(arrs)
    for bit in (4, 2, 1):
        step = bit * unit
        low = (lane & step) == 0
        for i in range(8):
            if i & bit:
                continue
            lo, hi = arrs[i], arrs[i | bit]
            arrs[i] = jnp.where(low, lo, pltpu.roll(hi, step, 1))
            arrs[i | bit] = jnp.where(low, pltpu.roll(lo, 128 - step, 1), hi)
    return arrs


def lane_blocks(shape, blocks):
    blk = lax.broadcasted_iota(jnp.int32, shape, 1) >> 4
    hit = blk == blocks[0]
    for b in blocks[1:]:
        hit = hit | (blk == b)
    return hit


def shift_row(w):
    row = lax.broadcasted_iota(jnp.int32, w.shape, 0)
    first = (row & 7) == 0
    prev = jnp.where(row < 128, 0.0, pltpu.roll(w, 121, 0))
    return jnp.where(first, prev, pltpu.roll(w, 1, 0))


def shift_depth(w):
    w = w.reshape(8, 16, 8, 128)
    even, odd = w[:, :8], w[:, 8:]
    back = jnp.concatenate([jnp.zeros_like(odd[:, :1]), odd[:, :7]], axis=1)
    return jnp.concatenate([back, even], axis=1).reshape(1024, 128)


def four_shifts(w_bf16):
    w = w_bf16.astype(F32).reshape(1024, 128)
    wj = shift_row(w)
    return [w.astype(BF16), shift_depth(w).astype(BF16), wj.astype(BF16), shift_depth(wj).astype(BF16)]


def selection(dj, dk):
    m = lax.broadcasted_iota(jnp.int32, (128, 256), 0)
    n = lax.broadcasted_iota(jnp.int32, (128, 256), 1)
    row = (m & 7) + dj
    k = 2 * ((m >> 3) & 7) + (m >> 6) + dk
    lane = (row >> 3) * 128 + (k & 1) * 64 + (k >> 1) * 8 + (row & 7)
    return jnp.where((n == lane) & (k < 16), 1.0, 0.0).astype(BF16)


def dot_t(x, y):
    return lax.dot_general(x, y, (((1,), (1,)), ((), ())), preferred_element_type=F32)


def body(
    vol_hbm, ker_hbm, grad_hbm, feat_out, ig_out, kg_out,
    vol, grad, vf, halo_b, halo_r, halo_c, vs, wbuf, gs, gtb, gnext, kall, rhs, rt, s1, asum, s2, own3, kb, fs, fb,
    pb, gv, igf,
    ins, snd_g, rcv_g, snd_v, rcv_v, snd_k, rcv_k, snd_h, rcv_h, snd_m, rcv_m, snd_2, rcv_2, snd_3, rcv_3,
    snd_f, rcv_f,
):
    s = lax.axis_index("space")
    f = lax.axis_index("filt")
    core = s % 2
    q = s // 2
    sib = s + 1 - 2 * core
    up = (s + 1) % NS
    down = (s + NS - 1) % NS
    fup = (f + 1) % NF
    fdown = (f + NF - 1) % NF
    dest = q // 2
    half = q % 2

    get_vol = pltpu.make_async_copy(vol_hbm, vol, ins.at[0])
    get_grad = pltpu.make_async_copy(grad_hbm, grad, ins.at[1])
    get_ker = pltpu.make_async_copy(ker_hbm.at[:, core], kall.at[f, core], ins.at[2])
    get_vol.start()
    get_grad.start()
    get_ker.start()

    barrier = pltpu.get_barrier_semaphore()
    hello = [(s, (f + i) % NF) for i in range(1, NF)]
    hello += [(sib, f), (down, f), (up, f), (down, fdown)]
    hello += [(2 * ((q + i) % NQ) + core, f) for i in range(1, NQ)]
    hello += [(2 * (2 * f + r) + core, (f + i) % NF) for r in range(2) for i in range(NF)]
    for dev in hello:
        pl.semaphore_signal(barrier, inc=1, device_id=dev, device_id_type=MESH)

    sent = []

    def copy(src, dst, ss, rs, dev):
        return pltpu.make_async_remote_copy(
            src_ref=src, dst_ref=dst, send_sem=ss, recv_sem=rs, device_id=dev, device_id_type=MESH
        )

    def send(*args):
        c = copy(*args)
        c.start()
        sent.append(c)

    def arrived(dst, ss, rs):
        copy(dst, dst, ss, rs, (sib, f)).wait_recv()

    get_vol.wait()
    for px in range(2):
        vf[pl.ds(((1 + px) * 17 + 1) * 32, 512), :] = vol[px].astype(F32).reshape(512, 128)
    parity = []
    for p in range(8):
        a, b, z = 1 + p // 4, 1 + (p // 2) % 2, p % 2
        parity.append(
            jnp.concatenate([vf[pl.ds((a * 17 + b) * 32 + 2 * k + z, 8, stride=64), :] for k in KS], axis=0)
        )
    for i, x in enumerate(swap_blocks(parity, 16)):
        vs[i] = x.astype(BF16)
    get_grad.wait()
    tiles = [
        jnp.concatenate([grad[2 * t].astype(F32), grad[2 * t + 1].astype(F32)], axis=1) for t in range(8)
    ]
    for i, x in enumerate(swap_blocks(tiles, 8)):
        gs[i] = x.astype(BF16)

    pl.semaphore_wait(barrier, len(hello))

    for i in range(1, NF):
        to = (f + i) % NF
        send(vs.at[to], wbuf.at[0, f], snd_v.at[i - 1], rcv_v.at[i - 1], (s, to))
    for i in range(1, NF):
        to = (f + i) % NF
        send(gs, gtb.at[f], snd_g.at[i - 1], rcv_g.at[i - 1], (s, to))
    wbuf[0, f] = vs[f]
    gtb[f] = gs[...]

    for i in range(1, NF):
        arrived(wbuf.at[0, (f + NF - i) % NF], snd_v.at[i - 1], rcv_v.at[i - 1])
    send(wbuf.at[0], wbuf.at[1], snd_m.at[0], rcv_m.at[0], (up, f))
    for i, x in enumerate(four_shifts(wbuf[0])):
        rhs[:, i * 128 : i * 128 + 128] = x
    for i in range(1, NF):
        arrived(gtb.at[(f + NF - i) % NF], snd_g.at[i - 1], rcv_g.at[i - 1])
    get_ker.wait()
    for i in range(1, NF):
        send(kall.at[f, core], kall.at[f, core], snd_k.at[i - 1], rcv_k.at[i - 1], (s, (f + i) % NF))
    gall = jnp.concatenate([gtb[:, t].reshape(256, 128) for t in range(8)], axis=1)
    own = jnp.dot(gall, rhs[...], preferred_element_type=F32)
    o = [own[:, i * 128 : i * 128 + 128] for i in range(4)]
    shape = (256, 128)
    rt[0] = o[0]
    rt[3] = jnp.where(lane_blocks(shape, (0, 4)), pltpu.roll(o[3], 16, 1), o[2])
    send(rt.at[3 * (1 - core)], s1.at[0], snd_m.at[3], rcv_m.at[3], (sib, f))
    send(vol.at[1], halo_b, snd_h.at[0], rcv_h.at[0], (up, f))
    send(vol.at[:, 15], halo_r, snd_h.at[1], rcv_h.at[1], (s, fup))
    send(vol.at[1, 15], halo_c, snd_h.at[2], rcv_h.at[2], (up, fup))
    send(gtb.at[:, f], gnext.at[0], snd_m.at[1], rcv_m.at[1], (down, f))
    send(gtb.at[:, fup], gnext.at[1], snd_m.at[2], rcv_m.at[2], (down, f))

    arrived(wbuf.at[1], snd_m.at[0], rcv_m.at[0])
    for i, x in enumerate(four_shifts(wbuf[1])):
        rhs[:, i * 128 : i * 128 + 128] = jnp.where(s > 0, x, jnp.zeros_like(x))
    below = jnp.dot(gall, rhs[...], preferred_element_type=F32)
    b = [below[:, i * 128 : i * 128 + 128] for i in range(4)]
    x = jnp.where(lane_blocks(shape, (4, 6)), pltpu.roll(b[1], 112, 1), o[1])
    rt[1] = jnp.where(lane_blocks(shape, (0,)), pltpu.roll(b[3], 16, 1), x)
    rt[2] = jnp.where(lane_blocks(shape, (0, 1)), pltpu.roll(b[2], 32, 1), b[0])
    send(rt.at[2 - core], s1.at[1], snd_m.at[4], rcv_m.at[4], (sib, f))

    for l in range(2):
        arrived(s1.at[l], snd_m.at[3 + l], rcv_m.at[3 + l])
        kept = 3 * core if l == 0 else 1 + core
        asum[l] = (rt[kept] + s1[l]).reshape(16, 16, 128)
        for i in range(1, NQ):
            qd = (q + i) % NQ
            n = 15 * l + i - 1
            send(asum.at[l, qd], s2.at[l, i - 1], snd_2.at[n], rcv_2.at[n], (2 * qd + core, f))

    homes = []
    for l in range(2):
        for i in range(1, NQ):
            n = 15 * l + i - 1
            arrived(s2.at[l, i - 1], snd_2.at[n], rcv_2.at[n])
        acc = asum[l, q]
        for i in range(1, NQ):
            acc = acc + s2[l, i - 1]
        own3[l] = acc
        kept = 3 * core if l == 0 else 1 + core
        slot = kb.at[f, kept, half]
        got = rcv_3.at[16 * l + 8 * half + f]
        for i in range(1, NQ):
            qd = (q + i) % NQ
            send(own3.at[l], slot, snd_3.at[16 * l + i], got, (2 * qd + core, dest))
        homes.append(copy(own3.at[l], slot, snd_3.at[16 * l], got, (s, dest)))

        @pl.when(f != dest)
        def _():
            homes[l].start()

        @pl.when(f == dest)
        def _():
            kb[f, kept, half] = own3[l]

    for i in range(1, NF):
        arrived(kall.at[(f + NF - i) % NF, core], snd_k.at[i - 1], rcv_k.at[i - 1])
    send(kall.at[:, core], kall.at[:, core], snd_m.at[5], rcv_m.at[5], (sib, f))

    arrived(halo_b, snd_h.at[0], rcv_h.at[0])
    arrived(halo_r, snd_h.at[1], rcv_h.at[1])
    arrived(halo_c, snd_h.at[2], rcv_h.at[2])
    low = halo_b[...].astype(F32).reshape(512, 128)
    vf[pl.ds(32, 512), :] = jnp.where(s > 0, low, jnp.zeros_like(low))
    edge = halo_c[...].astype(F32)
    vf[pl.ds(0, 32), :] = jnp.where((s > 0) & (f > 0), edge, jnp.zeros_like(edge))
    for px in range(2):
        edge = halo_r[px].astype(F32)
        vf[pl.ds((1 + px) * 17 * 32, 32), :] = jnp.where(f > 0, edge, jnp.zeros_like(edge))
    for a in range(3):
        for b3 in range(3):
            def cells(z):
                return vf[pl.ds((a * 17 + b3) * 32 + z, 8, stride=64), :]
            for c in range(3):
                col = ((a * 3 + b3) * 3 + c) * 128
                rows = [
                    jnp.zeros((8, 128), F32) if 2 * k + c == 0 else cells(2 * k + c - 1) for k in KS
                ]
                pb[:, col : col + 128] = jnp.concatenate(rows, axis=0).astype(BF16)

    def tap(n):
        return kall[:, :, n].reshape(256, 128)

    arrived(kall.at[:, 1 - core], snd_m.at[5], rcv_m.at[5])
    total = jnp.zeros((256, 128), F32)
    for a in range(3):
        taps = jnp.concatenate([tap(9 * a + n) for n in range(9)], axis=1)
        total = total + dot_t(taps, pb[:, 1152 * a : 1152 * a + 1152])
    fs[...] = total.astype(BF16).reshape(8, 32, 128)
    for i in range(1, NF):
        to = (f + i) % NF
        send(fs.at[to], fb.at[f], snd_f.at[i - 1], rcv_f.at[i - 1], (s, to))
    fb[f] = fs[f]

    arrived(gnext.at[0], snd_m.at[1], rcv_m.at[1])
    arrived(gnext.at[1], snd_m.at[2], rcv_m.at[2])
    picks = jnp.concatenate([selection(dj, dk) for dj in range(2) for dk in range(2)], axis=0)
    here = gtb[:, f].reshape(256, 128)
    nxt = gtb[:, fup].reshape(256, 128)
    nxt = jnp.where(f < NF - 1, nxt, jnp.zeros_like(nxt))
    gv[0] = dot_t(picks, jnp.concatenate([here, nxt], axis=1)).astype(BF16)
    here = gnext[0].reshape(256, 128)
    here = jnp.where(s < NS - 1, here, jnp.zeros_like(here))
    nxt = gnext[1].reshape(256, 128)
    nxt = jnp.where((s < NS - 1) & (f < NF - 1), nxt, jnp.zeros_like(nxt))
    gv[1] = dot_t(picks, jnp.concatenate([here, nxt], axis=1)).astype(BF16)
    steps = (((1, 0),), ((0, 1), (2, 0)))
    for px in range(2):
        for py in range(2):
            for pz in range(2):
                left, right = [], []
                for a, di in steps[px]:
                    for b3, dj in steps[py]:
                        for c, dk in steps[pz]:
                            v = (2 * dj + dk) * 128
                            left.append(gv[di, v : v + 128])
                            right.append(tap(9 * a + 3 * b3 + c))
                res = jnp.dot(
                    jnp.concatenate(left, axis=1), jnp.concatenate(right, axis=0), preferred_element_type=F32
                )
                for n, k in enumerate(KS):
                    igf[pl.ds((px * 16 + py) * 32 + 2 * k + pz, 8, stride=64), :] = res[8 * n : 8 * n + 8]
    ig_out[...] = igf[...].reshape(2, 16, 32, 128).astype(BF16)

    for l in range(2):
        kept = 3 * core if l == 0 else 1 + core
        for r in range(2):
            for i in range(NF):
                src = (f + i) % NF
                got = copy(
                    own3.at[l], kb.at[src, kept, r], snd_3.at[0], rcv_3.at[16 * l + 8 * r + src], (sib, f)
                )
                if i == 0:
                    @pl.when(2 * f + r != q)
                    def _():
                        got.wait_recv()
                else:
                    got.wait_recv()
        send(kb.at[:, kept], kb.at[:, kept], snd_m.at[6 + l], rcv_m.at[6 + l], (sib, f))

    for i in range(1, NF):
        arrived(fb.at[(f + NF - i) % NF], snd_f.at[i - 1], rcv_f.at[i - 1])
    for t, x in enumerate(swap_blocks([fb[i].astype(F32) for i in range(8)], 8)):
        feat_out[2 * t] = x[:, :64].astype(BF16)
        feat_out[2 * t + 1] = x[:, 64:].astype(BF16)

    factor = float(32 * 64 * 16) ** -0.5
    for l in range(2):
        arrived(kb.at[:, 3 * (1 - core) if l == 0 else 2 - core], snd_m.at[6 + l], rcv_m.at[6 + l])
        for lt in ((0, 3), (1, 2))[l]:
            blocks = swap_blocks([kb[i, lt].reshape(32, 128) for i in range(8)], 16)
            for pos in range(8):
                if (lt, pos) in TAPS:
                    a, b3, c = TAPS[(lt, pos)]
                    kg_out[9 * a + 3 * b3 + c] = blocks[pos] * factor

    for c in sent:
        c.wait_send()
    for c in homes:
        @pl.when(f != dest)
        def _():
            c.wait_send()


def on_device(volume, kernel, out_grad):
    vmem = pl.BlockSpec(memory_space=pltpu.VMEM)
    hbm = pl.BlockSpec(memory_space=pltpu.HBM)
    dma = pltpu.SemaphoreType.DMA
    inputs = (volume, kernel.reshape(27, 2, 16, 128), out_grad.transpose(0, 2, 3, 1).reshape(16, 32, 64))
    feat, ig, kg = pl.pallas_call(
        body,
        out_shape=(
            jax.ShapeDtypeStruct((16, 32, 64), BF16),
            jax.ShapeDtypeStruct((2, 16, 32, 128), BF16),
            jax.ShapeDtypeStruct((27, 32, 128), F32),
        ),
        in_specs=[hbm] * 3,
        out_specs=(vmem,) * 3,
        scratch_shapes=[
            pltpu.VMEM((2, 16, 32, 128), BF16),
            pltpu.VMEM((16, 32, 64), BF16),
            pltpu.VMEM((3 * 17 * 32, 128), F32),
            pltpu.VMEM((16, 32, 128), BF16),
            pltpu.VMEM((2, 32, 128), BF16),
            pltpu.VMEM((32, 128), BF16),
            pltpu.VMEM((8, 128, 128), BF16),
            pltpu.VMEM((2, 8, 128, 128), BF16),
            pltpu.VMEM((8, 32, 128), BF16),
            pltpu.VMEM((8, 8, 32, 128), BF16),
            pltpu.VMEM((2, 8, 32, 128), BF16),
            pltpu.VMEM((8, 2, 27, 16, 128), BF16),
            pltpu.VMEM((1024, 512), BF16),
            pltpu.VMEM((4, 256, 128), F32),
            pltpu.VMEM((2, 256, 128), F32),
            pltpu.VMEM((2, 16, 16, 128), F32),
            pltpu.VMEM((2, 15, 16, 128), F32),
            pltpu.VMEM((2, 16, 128), F32),
            pltpu.VMEM((8, 4, 2, 16, 128), F32),
            pltpu.VMEM((8, 32, 128), BF16),
            pltpu.VMEM((8, 32, 128), BF16),
            pltpu.VMEM((128, 27 * 128), BF16),
            pltpu.VMEM((2, 512, 256), BF16),
            pltpu.VMEM((2 * 16 * 32, 128), F32),
            dma((3,)),
            dma((7,)), dma((7,)), dma((7,)), dma((7,)), dma((7,)), dma((7,)),
            dma((3,)), dma((3,)), dma((8,)), dma((8,)), dma((30,)), dma((30,)),
            dma((32,)), dma((32,)), dma((7,)), dma((7,)),
        ],
        compiler_params=pltpu.CompilerParams(
            collective_id=0, has_side_effects=True, vmem_limit_bytes=40 * 1024 * 1024
        ),
        name="conv_fwd_bwd",
    )(*[pltpu.with_memory_space_constraint(x, pltpu.HBM) for x in inputs])
    features = feat.reshape(1, 16, 32, 64).transpose(0, 3, 1, 2)
    return features, ig, kg.reshape(3, 3, 3, 32, 128)


def solution(mesh):
    return jax.shard_map(
        on_device,
        mesh=mesh,
        in_specs=(
            P("space", "filt", None, None),
            P(None, None, None, "filt", None),
            P("space", None, None, "filt"),
        ),
        out_specs=(
            P("space", None, None, "filt"),
            P("space", "filt", None, None),
            P(None, None, None, "filt", None),
        ),
        check_vma=False,
    )
```

```python
import jax
import jax.numpy as jnp
from jax import lax
from jax.experimental import pallas as pl
from jax.experimental.pallas import tpu as pltpu
from jax.sharding import PartitionSpec as P

MESH = pl.DeviceIdType.MESH
F32 = jnp.float32
BF16 = jnp.bfloat16
NF = 8
NS = 32
NQ = 16
FAR = (8, 7, 9, 6, 10, 5, 11, 4, 12, 3, 13, 2, 14, 1, 15)
KS = [2 * t + e for e in range(2) for t in range(8)]

TAPS = {}
for _p in range(8):
    _x, _y, _z = _p // 4, (_p // 2) % 2, _p % 2
    TAPS[(0, _p)] = (1 + _x, 1 + _y, 1 + _z)
    if _z:
        TAPS[(1, _p)] = (1 + _x, 1 + _y, 0)
    if _x:
        TAPS[(2, _p)] = (0, 1 + _y, 1 + _z)
    if _y:
        TAPS[(3, _p)] = (1 + _x, 0, 1 + _z)
TAPS[(1, 4)] = (0, 1, 0)
TAPS[(1, 6)] = (0, 2, 0)
TAPS[(1, 0)] = (0, 0, 0)
TAPS[(2, 0)] = (0, 0, 1)
TAPS[(2, 1)] = (0, 0, 2)
TAPS[(3, 4)] = (1, 0, 0)
TAPS[(3, 0)] = (2, 0, 0)


def swap_blocks(arrs, unit):
    lane = lax.broadcasted_iota(jnp.int32, arrs[0].shape, 1)
    arrs = list(arrs)
    for bit in (4, 2, 1):
        step = bit * unit
        low = (lane & step) == 0
        for i in range(8):
            if i & bit:
                continue
            lo, hi = arrs[i], arrs[i | bit]
            arrs[i] = jnp.where(low, lo, pltpu.roll(hi, step, 1))
            arrs[i | bit] = jnp.where(low, pltpu.roll(lo, 128 - step, 1), hi)
    return arrs


def lane_blocks(shape, blocks):
    blk = lax.broadcasted_iota(jnp.int32, shape, 1) >> 4
    hit = blk == blocks[0]
    for b in blocks[1:]:
        hit = hit | (blk == b)
    return hit


def shift_row(w):
    row = lax.broadcasted_iota(jnp.int32, w.shape, 0)
    first = (row & 7) == 0
    prev = jnp.where(row < 128, 0.0, pltpu.roll(w, 121, 0))
    return jnp.where(first, prev, pltpu.roll(w, 1, 0))


def shift_depth(w):
    w = w.reshape(8, 16, 8, 128)
    even, odd = w[:, :8], w[:, 8:]
    back = jnp.concatenate([jnp.zeros_like(odd[:, :1]), odd[:, :7]], axis=1)
    return jnp.concatenate([back, even], axis=1).reshape(1024, 128)


def four_shifts(w_bf16):
    w = w_bf16.astype(F32).reshape(1024, 128)
    wj = shift_row(w)
    return [w.astype(BF16), shift_depth(w).astype(BF16), wj.astype(BF16), shift_depth(wj).astype(BF16)]


def selection(dj, dk):
    m = lax.broadcasted_iota(jnp.int32, (128, 256), 0)
    n = lax.broadcasted_iota(jnp.int32, (128, 256), 1)
    row = (m & 7) + dj
    k = 2 * ((m >> 3) & 7) + (m >> 6) + dk
    lane = (row >> 3) * 128 + (k & 1) * 64 + (k >> 1) * 8 + (row & 7)
    return jnp.where((n == lane) & (k < 16), 1.0, 0.0).astype(BF16)


def dot_t(x, y):
    return lax.dot_general(x, y, (((1,), (1,)), ((), ())), preferred_element_type=F32)


def body(
    vol_hbm, ker_hbm, grad_hbm, feat_out, ig_out, kg_out,
    vol, grad, vf, halo_b, halo_r, halo_c, vs, wbuf, gs, gtb, gnext, kall, rhs, rt, s1, asum, s2, own3, kb, fs, fb,
    pb, gv, igf,
    ins, snd_g, rcv_g, snd_v, rcv_v, snd_k, rcv_k, snd_h, rcv_h, snd_m, rcv_m, snd_2, rcv_2, snd_3, rcv_3,
    snd_f, rcv_f,
):
    s = lax.axis_index("space")
    f = lax.axis_index("filt")
    core = s % 2
    q = s // 2
    sib = s + 1 - 2 * core
    sx = s + 2 - 4 * (q % 2)
    fx = f + 1 - 2 * (f % 2)
    up = (s + 1) % NS
    down = (s + NS - 1) % NS
    fup = (f + 1) % NF
    fdown = (f + NF - 1) % NF
    dest = q // 2
    half = q % 2

    get_vol = pltpu.make_async_copy(vol_hbm, vol, ins.at[0])
    get_grad = pltpu.make_async_copy(grad_hbm, grad, ins.at[1])
    get_ker = pltpu.make_async_copy(ker_hbm.at[:, core], kall.at[f, core], ins.at[2])
    get_vol.start()
    get_grad.start()
    get_ker.start()

    barrier = pltpu.get_barrier_semaphore()
    hello = [(s, (f + i) % NF) for i in range(1, NF)]
    hello += [(sx, fx), (sib, f), (down, f), (up, f), (down, fdown)]
    hello += [(2 * ((q + i) % NQ) + core, f) for i in range(1, NQ)]
    hello += [(2 * (2 * f + r) + core, (f + i) % NF) for r in range(2) for i in range(NF)]
    for dev in hello:
        pl.semaphore_signal(barrier, inc=1, device_id=dev, device_id_type=MESH)

    sent = []

    def copy(src, dst, ss, rs, dev):
        return pltpu.make_async_remote_copy(
            src_ref=src, dst_ref=dst, send_sem=ss, recv_sem=rs, device_id=dev, device_id_type=MESH
        )

    def send(*args):
        c = copy(*args)
        c.start()
        sent.append(c)

    def arrived(dst, ss, rs):
        copy(dst, dst, ss, rs, (sib, f)).wait_recv()

    get_vol.wait()
    for px in range(2):
        vf[pl.ds(((1 + px) * 17 + 1) * 32, 512), :] = vol[px].astype(F32).reshape(512, 128)
    parity = []
    for p in range(8):
        a, b, z = 1 + p // 4, 1 + (p // 2) % 2, p % 2
        parity.append(
            jnp.concatenate([vf[pl.ds((a * 17 + b) * 32 + 2 * k + z, 8, stride=64), :] for k in KS], axis=0)
        )
    for i, x in enumerate(swap_blocks(parity, 16)):
        vs[i] = x.astype(BF16)
    get_grad.wait()
    tiles = [
        jnp.concatenate([grad[2 * t].astype(F32), grad[2 * t + 1].astype(F32)], axis=1) for t in range(8)
    ]
    for i, x in enumerate(swap_blocks(tiles, 8)):
        gs[i] = x.astype(BF16)

    pl.semaphore_wait(barrier, len(hello))

    send(gs, gtb.at[f], snd_g.at[0], rcv_g.at[0], (s, fx))
    for i in range(1, NF):
        to = (f + i) % NF
        send(vs.at[to], wbuf.at[0, f], snd_v.at[i - 1], rcv_v.at[i - 1], (s, to))
    for i in range(1, 4):
        send(gs, gtb.at[f], snd_g.at[i], rcv_g.at[i], (s, (f + 2 * i) % NF))
    wbuf[0, f] = vs[f]
    gtb[f] = gs[...]

    get_ker.wait()
    send(kall.at[f, core], kall.at[f, core], snd_k.at[0], rcv_k.at[0], (sx, fx))
    arrived(gtb.at[fx], snd_g.at[0], rcv_g.at[0])
    for i in range(1, 4):
        send(gtb.at[fx], gtb.at[fx], snd_g.at[3 + i], rcv_g.at[3 + i], (s, (f + 2 * i) % NF))

    for i in range(1, NF):
        arrived(wbuf.at[0, (f + NF - i) % NF], snd_v.at[i - 1], rcv_v.at[i - 1])
    send(wbuf.at[0], wbuf.at[1], snd_m.at[0], rcv_m.at[0], (up, f))
    for i, x in enumerate(four_shifts(wbuf[0])):
        rhs[:, i * 128 : i * 128 + 128] = x
    for i in range(1, 4):
        arrived(gtb.at[(f + NF - 2 * i) % NF], snd_g.at[i], rcv_g.at[i])
    for i in range(1, 4):
        arrived(gtb.at[(fx + NF - 2 * i) % NF], snd_g.at[3 + i], rcv_g.at[3 + i])
    arrived(kall.at[fx, core], snd_k.at[0], rcv_k.at[0])
    for n, by in enumerate((2, 6)):
        to = (s, (f + by) % NF)
        send(kall.at[f, core], kall.at[f, core], snd_k.at[1 + n], rcv_k.at[1 + n], to)
        send(kall.at[fx, core], kall.at[fx, core], snd_k.at[3 + n], rcv_k.at[3 + n], to)
    gall = jnp.concatenate([gtb[:, t].reshape(256, 128) for t in range(8)], axis=1)
    own = jnp.dot(gall, rhs[...], preferred_element_type=F32)
    o = [own[:, i * 128 : i * 128 + 128] for i in range(4)]
    shape = (256, 128)
    rt[0] = o[0]
    rt[3] = jnp.where(lane_blocks(shape, (0, 4)), pltpu.roll(o[3], 16, 1), o[2])
    send(rt.at[3 * (1 - core)], s1.at[0], snd_m.at[3], rcv_m.at[3], (sib, f))
    send(vol.at[1], halo_b, snd_h.at[0], rcv_h.at[0], (up, f))
    send(vol.at[:, 15], halo_r, snd_h.at[1], rcv_h.at[1], (s, fup))
    send(vol.at[1, 15], halo_c, snd_h.at[2], rcv_h.at[2], (up, fup))
    send(gtb.at[:, f], gnext.at[0], snd_m.at[1], rcv_m.at[1], (down, f))
    send(gtb.at[:, fup], gnext.at[1], snd_m.at[2], rcv_m.at[2], (down, f))

    arrived(wbuf.at[1], snd_m.at[0], rcv_m.at[0])
    for i, x in enumerate(four_shifts(wbuf[1])):
        rhs[:, i * 128 : i * 128 + 128] = jnp.where(s > 0, x, jnp.zeros_like(x))
    below = jnp.dot(gall, rhs[...], preferred_element_type=F32)
    b = [below[:, i * 128 : i * 128 + 128] for i in range(4)]
    x = jnp.where(lane_blocks(shape, (4, 6)), pltpu.roll(b[1], 112, 1), o[1])
    rt[1] = jnp.where(lane_blocks(shape, (0,)), pltpu.roll(b[3], 16, 1), x)
    rt[2] = jnp.where(lane_blocks(shape, (0, 1)), pltpu.roll(b[2], 32, 1), b[0])
    send(rt.at[2 - core], s1.at[1], snd_m.at[4], rcv_m.at[4], (sib, f))

    for l in range(2):
        arrived(s1.at[l], snd_m.at[3 + l], rcv_m.at[3 + l])
        kept = 3 * core if l == 0 else 1 + core
        asum[l] = (rt[kept] + s1[l]).reshape(16, 16, 128)
        for i in FAR:
            qd = (q + i) % NQ
            n = 15 * l + i - 1
            send(asum.at[l, qd], s2.at[l, i - 1], snd_2.at[n], rcv_2.at[n], (2 * qd + core, f))

    arrived(kall.at[(f + 6) % NF, core], snd_k.at[1], rcv_k.at[1])
    send(kall.at[(f + 6) % NF, core], kall.at[(f + 6) % NF, core], snd_k.at[5], rcv_k.at[5], (s, (f + 2) % NF))
    arrived(kall.at[(fx + 2) % NF, core], snd_k.at[4], rcv_k.at[4])
    send(kall.at[(fx + 2) % NF, core], kall.at[(fx + 2) % NF, core], snd_k.at[6], rcv_k.at[6], (s, (f + 6) % NF))

    homes = []
    for l in range(2):
        for i in range(1, NQ):
            n = 15 * l + i - 1
            arrived(s2.at[l, i - 1], snd_2.at[n], rcv_2.at[n])
        acc = asum[l, q]
        for i in range(1, NQ):
            acc = acc + s2[l, i - 1]
        own3[l] = acc
        kept = 3 * core if l == 0 else 1 + core
        slot = kb.at[f, kept, half]
        got = rcv_3.at[16 * l + 8 * half + f]
        for i in FAR:
            qd = (q + i) % NQ
            send(own3.at[l], slot, snd_3.at[16 * l + i], got, (2 * qd + core, dest))
        homes.append(copy(own3.at[l], slot, snd_3.at[16 * l], got, (s, dest)))

        @pl.when(f != dest)
        def _():
            homes[l].start()

        @pl.when(f == dest)
        def _():
            kb[f, kept, half] = own3[l]

    arrived(kall.at[(f + 2) % NF, core], snd_k.at[2], rcv_k.at[2])
    arrived(kall.at[(fx + 6) % NF, core], snd_k.at[3], rcv_k.at[3])
    arrived(kall.at[(f + 4) % NF, core], snd_k.at[5], rcv_k.at[5])
    arrived(kall.at[(fx + 4) % NF, core], snd_k.at[6], rcv_k.at[6])
    send(kall.at[:, core], kall.at[:, core], snd_m.at[5], rcv_m.at[5], (sib, f))

    arrived(halo_b, snd_h.at[0], rcv_h.at[0])
    arrived(halo_r, snd_h.at[1], rcv_h.at[1])
    arrived(halo_c, snd_h.at[2], rcv_h.at[2])
    low = halo_b[...].astype(F32).reshape(512, 128)
    vf[pl.ds(32, 512), :] = jnp.where(s > 0, low, jnp.zeros_like(low))
    edge = halo_c[...].astype(F32)
    vf[pl.ds(0, 32), :] = jnp.where((s > 0) & (f > 0), edge, jnp.zeros_like(edge))
    for px in range(2):
        edge = halo_r[px].astype(F32)
        vf[pl.ds((1 + px) * 17 * 32, 32), :] = jnp.where(f > 0, edge, jnp.zeros_like(edge))
    for a in range(3):
        for b3 in range(3):
            def cells(z):
                return vf[pl.ds((a * 17 + b3) * 32 + z, 8, stride=64), :]
            for c in range(3):
                col = ((a * 3 + b3) * 3 + c) * 128
                rows = [
                    jnp.zeros((8, 128), F32) if 2 * k + c == 0 else cells(2 * k + c - 1) for k in KS
                ]
                pb[:, col : col + 128] = jnp.concatenate(rows, axis=0).astype(BF16)

    def tap(n):
        return kall[:, :, n].reshape(256, 128)

    arrived(kall.at[:, 1 - core], snd_m.at[5], rcv_m.at[5])
    total = jnp.zeros((256, 128), F32)
    for a in range(3):
        taps = jnp.concatenate([tap(9 * a + n) for n in range(9)], axis=1)
        total = total + dot_t(taps, pb[:, 1152 * a : 1152 * a + 1152])
    fs[...] = total.astype(BF16).reshape(8, 32, 128)
    for i in range(1, NF):
        to = (f + i) % NF
        send(fs.at[to], fb.at[f], snd_f.at[i - 1], rcv_f.at[i - 1], (s, to))
    fb[f] = fs[f]

    arrived(gnext.at[0], snd_m.at[1], rcv_m.at[1])
    arrived(gnext.at[1], snd_m.at[2], rcv_m.at[2])
    picks = jnp.concatenate([selection(dj, dk) for dj in range(2) for dk in range(2)], axis=0)
    here = gtb[:, f].reshape(256, 128)
    nxt = gtb[:, fup].reshape(256, 128)
    nxt = jnp.where(f < NF - 1, nxt, jnp.zeros_like(nxt))
    gv[0] = dot_t(picks, jnp.concatenate([here, nxt], axis=1)).astype(BF16)
    here = gnext[0].reshape(256, 128)
    here = jnp.where(s < NS - 1, here, jnp.zeros_like(here))
    nxt = gnext[1].reshape(256, 128)
    nxt = jnp.where((s < NS - 1) & (f < NF - 1), nxt, jnp.zeros_like(nxt))
    gv[1] = dot_t(picks, jnp.concatenate([here, nxt], axis=1)).astype(BF16)
    steps = (((1, 0),), ((0, 1), (2, 0)))
    for px in range(2):
        for py in range(2):
            for pz in range(2):
                left, right = [], []
                for a, di in steps[px]:
                    for b3, dj in steps[py]:
                        for c, dk in steps[pz]:
                            v = (2 * dj + dk) * 128
                            left.append(gv[di, v : v + 128])
                            right.append(tap(9 * a + 3 * b3 + c))
                res = jnp.dot(
                    jnp.concatenate(left, axis=1), jnp.concatenate(right, axis=0), preferred_element_type=F32
                )
                for n, k in enumerate(KS):
                    igf[pl.ds((px * 16 + py) * 32 + 2 * k + pz, 8, stride=64), :] = res[8 * n : 8 * n + 8]
    ig_out[...] = igf[...].reshape(2, 16, 32, 128).astype(BF16)

    for l in range(2):
        kept = 3 * core if l == 0 else 1 + core
        for r in range(2):
            for i in range(NF):
                src = (f + i) % NF
                got = copy(
                    own3.at[l], kb.at[src, kept, r], snd_3.at[0], rcv_3.at[16 * l + 8 * r + src], (sib, f)
                )
                if i == 0:
                    @pl.when(2 * f + r != q)
                    def _():
                        got.wait_recv()
                else:
                    got.wait_recv()
        send(kb.at[:, kept], kb.at[:, kept], snd_m.at[6 + l], rcv_m.at[6 + l], (sib, f))

    for i in range(1, NF):
        arrived(fb.at[(f + NF - i) % NF], snd_f.at[i - 1], rcv_f.at[i - 1])
    for t, x in enumerate(swap_blocks([fb[i].astype(F32) for i in range(8)], 8)):
        feat_out[2 * t] = x[:, :64].astype(BF16)
        feat_out[2 * t + 1] = x[:, 64:].astype(BF16)

    factor = float(32 * 64 * 16) ** -0.5
    for l in range(2):
        arrived(kb.at[:, 3 * (1 - core) if l == 0 else 2 - core], snd_m.at[6 + l], rcv_m.at[6 + l])
        for lt in ((0, 3), (1, 2))[l]:
            blocks = swap_blocks([kb[i, lt].reshape(32, 128) for i in range(8)], 16)
            for pos in range(8):
                if (lt, pos) in TAPS:
                    a, b3, c = TAPS[(lt, pos)]
                    kg_out[9 * a + 3 * b3 + c] = blocks[pos] * factor

    for c in sent:
        c.wait_send()
    for c in homes:
        @pl.when(f != dest)
        def _():
            c.wait_send()


def on_device(volume, kernel, out_grad):
    vmem = pl.BlockSpec(memory_space=pltpu.VMEM)
    hbm = pl.BlockSpec(memory_space=pltpu.HBM)
    dma = pltpu.SemaphoreType.DMA
    inputs = (volume, kernel.reshape(27, 2, 16, 128), out_grad.transpose(0, 2, 3, 1).reshape(16, 32, 64))
    feat, ig, kg = pl.pallas_call(
        body,
        out_shape=(
            jax.ShapeDtypeStruct((16, 32, 64), BF16),
            jax.ShapeDtypeStruct((2, 16, 32, 128), BF16),
            jax.ShapeDtypeStruct((27, 32, 128), F32),
        ),
        in_specs=[hbm] * 3,
        out_specs=(vmem,) * 3,
        scratch_shapes=[
            pltpu.VMEM((2, 16, 32, 128), BF16),
            pltpu.VMEM((16, 32, 64), BF16),
            pltpu.VMEM((3 * 17 * 32, 128), F32),
            pltpu.VMEM((16, 32, 128), BF16),
            pltpu.VMEM((2, 32, 128), BF16),
            pltpu.VMEM((32, 128), BF16),
            pltpu.VMEM((8, 128, 128), BF16),
            pltpu.VMEM((2, 8, 128, 128), BF16),
            pltpu.VMEM((8, 32, 128), BF16),
            pltpu.VMEM((8, 8, 32, 128), BF16),
            pltpu.VMEM((2, 8, 32, 128), BF16),
            pltpu.VMEM((8, 2, 27, 16, 128), BF16),
            pltpu.VMEM((1024, 512), BF16),
            pltpu.VMEM((4, 256, 128), F32),
            pltpu.VMEM((2, 256, 128), F32),
            pltpu.VMEM((2, 16, 16, 128), F32),
            pltpu.VMEM((2, 15, 16, 128), F32),
            pltpu.VMEM((2, 16, 128), F32),
            pltpu.VMEM((8, 4, 2, 16, 128), F32),
            pltpu.VMEM((8, 32, 128), BF16),
            pltpu.VMEM((8, 32, 128), BF16),
            pltpu.VMEM((128, 27 * 128), BF16),
            pltpu.VMEM((2, 512, 256), BF16),
            pltpu.VMEM((2 * 16 * 32, 128), F32),
            dma((3,)),
            dma((7,)), dma((7,)), dma((7,)), dma((7,)), dma((7,)), dma((7,)),
            dma((3,)), dma((3,)), dma((8,)), dma((8,)), dma((30,)), dma((30,)),
            dma((32,)), dma((32,)), dma((7,)), dma((7,)),
        ],
        compiler_params=pltpu.CompilerParams(
            collective_id=0, has_side_effects=True, vmem_limit_bytes=40 * 1024 * 1024
        ),
        name="conv_fwd_bwd",
    )(*[pltpu.with_memory_space_constraint(x, pltpu.HBM) for x in inputs])
    features = feat.reshape(1, 16, 32, 64).transpose(0, 3, 1, 2)
    return features, ig, kg.reshape(3, 3, 3, 32, 128)


def solution(mesh):
    return jax.shard_map(
        on_device,
        mesh=mesh,
        in_specs=(
            P("space", "filt", None, None),
            P(None, None, None, "filt", None),
            P("space", None, None, "filt"),
        ),
        out_specs=(
            P("space", None, None, "filt"),
            P("space", "filt", None, None),
            P(None, None, None, "filt", None),
        ),
        check_vma=False,
    )
```

```python
import jax
import jax.numpy as jnp
from jax import lax
from jax.experimental import pallas as pl
from jax.experimental.pallas import tpu as pltpu
from jax.sharding import PartitionSpec as P

MESH = pl.DeviceIdType.MESH
F32 = jnp.float32
BF16 = jnp.bfloat16
NF = 8
NS = 32
NQ = 16
FAR = (8, 7, 9, 6, 10, 5, 11, 4, 12, 3, 13, 2, 14, 1, 15)
KS = [2 * t + e for e in range(2) for t in range(8)]

TAPS = {}
for _p in range(8):
    _x, _y, _z = _p // 4, (_p // 2) % 2, _p % 2
    TAPS[(0, _p)] = (1 + _x, 1 + _y, 1 + _z)
    if _z:
        TAPS[(1, _p)] = (1 + _x, 1 + _y, 0)
    if _x:
        TAPS[(2, _p)] = (0, 1 + _y, 1 + _z)
    if _y:
        TAPS[(3, _p)] = (1 + _x, 0, 1 + _z)
TAPS[(1, 4)] = (0, 1, 0)
TAPS[(1, 6)] = (0, 2, 0)
TAPS[(1, 0)] = (0, 0, 0)
TAPS[(2, 0)] = (0, 0, 1)
TAPS[(2, 1)] = (0, 0, 2)
TAPS[(3, 4)] = (1, 0, 0)
TAPS[(3, 0)] = (2, 0, 0)


def swap_blocks(arrs, unit):
    lane = lax.broadcasted_iota(jnp.int32, arrs[0].shape, 1)
    arrs = list(arrs)
    for bit in (4, 2, 1):
        step = bit * unit
        low = (lane & step) == 0
        for i in range(8):
            if i & bit:
                continue
            lo, hi = arrs[i], arrs[i | bit]
            arrs[i] = jnp.where(low, lo, pltpu.roll(hi, step, 1))
            arrs[i | bit] = jnp.where(low, pltpu.roll(lo, 128 - step, 1), hi)
    return arrs


def lane_blocks(shape, blocks):
    blk = lax.broadcasted_iota(jnp.int32, shape, 1) >> 4
    hit = blk == blocks[0]
    for b in blocks[1:]:
        hit = hit | (blk == b)
    return hit


def shift_row(w):
    row = lax.broadcasted_iota(jnp.int32, w.shape, 0)
    first = (row & 7) == 0
    prev = jnp.where(row < 128, 0.0, pltpu.roll(w, 121, 0))
    return jnp.where(first, prev, pltpu.roll(w, 1, 0))


def shift_depth(w):
    w = w.reshape(8, 16, 8, 128)
    even, odd = w[:, :8], w[:, 8:]
    back = jnp.concatenate([jnp.zeros_like(odd[:, :1]), odd[:, :7]], axis=1)
    return jnp.concatenate([back, even], axis=1).reshape(1024, 128)


def four_shifts(w_bf16):
    w = w_bf16.astype(F32).reshape(1024, 128)
    wj = shift_row(w)
    return [w.astype(BF16), shift_depth(w).astype(BF16), wj.astype(BF16), shift_depth(wj).astype(BF16)]


def selection(dj, dk):
    m = lax.broadcasted_iota(jnp.int32, (128, 256), 0)
    n = lax.broadcasted_iota(jnp.int32, (128, 256), 1)
    row = (m & 7) + dj
    k = 2 * ((m >> 3) & 7) + (m >> 6) + dk
    lane = (row >> 3) * 128 + (k & 1) * 64 + (k >> 1) * 8 + (row & 7)
    return jnp.where((n == lane) & (k < 16), 1.0, 0.0).astype(BF16)


def dot_t(x, y):
    return lax.dot_general(x, y, (((1,), (1,)), ((), ())), preferred_element_type=F32)


def body(
    vol_hbm, ker_hbm, grad_hbm, feat_out, ig_out, kg_out,
    vol, grad, vf, halo_b, halo_r, halo_c, vs, wbuf, gs, gtb, gnext, kall, rhs, rt, s1, asum, s2, own3, kb, fs, fb,
    pb, gv, igf,
    ins, snd_g, rcv_g, snd_v, rcv_v, snd_k, rcv_k, snd_h, rcv_h, snd_m, rcv_m, snd_2, rcv_2, snd_3, rcv_3,
    snd_f, rcv_f,
):
    s = lax.axis_index("space")
    f = lax.axis_index("filt")
    core = s % 2
    q = s // 2
    sib = s + 1 - 2 * core
    sx = s + 2 - 4 * (q % 2)
    fx = f + 1 - 2 * (f % 2)
    up = (s + 1) % NS
    down = (s + NS - 1) % NS
    fup = (f + 1) % NF
    fdown = (f + NF - 1) % NF
    dest = q // 2
    half = q % 2

    get_vol = pltpu.make_async_copy(vol_hbm, vol, ins.at[0])
    get_grad = pltpu.make_async_copy(grad_hbm, grad, ins.at[1])
    get_ker = pltpu.make_async_copy(ker_hbm.at[:, core], kall.at[f, core], ins.at[2])
    get_vol.start()
    get_grad.start()
    get_ker.start()

    barrier = pltpu.get_barrier_semaphore()
    hello = [(s, (f + i) % NF) for i in range(1, NF)]
    hello += [(sx, fx), (sib, f), (down, f), (up, f), (down, fdown)]
    hello += [(2 * ((q + i) % NQ) + core, f) for i in range(1, NQ)]
    hello += [(2 * (2 * f + r) + core, (f + i) % NF) for r in range(2) for i in range(NF)]
    for dev in hello:
        pl.semaphore_signal(barrier, inc=1, device_id=dev, device_id_type=MESH)

    sent = []

    def copy(src, dst, ss, rs, dev):
        return pltpu.make_async_remote_copy(
            src_ref=src, dst_ref=dst, send_sem=ss, recv_sem=rs, device_id=dev, device_id_type=MESH
        )

    def send(*args):
        c = copy(*args)
        c.start()
        sent.append(c)

    def arrived(dst, ss, rs):
        copy(dst, dst, ss, rs, (sib, f)).wait_recv()

    get_vol.wait()
    for px in range(2):
        vf[pl.ds(((1 + px) * 17 + 1) * 32, 512), :] = vol[px].astype(F32).reshape(512, 128)
    parity = []
    for p in range(8):
        a, b, z = 1 + p // 4, 1 + (p // 2) % 2, p % 2
        parity.append(
            jnp.concatenate([vf[pl.ds((a * 17 + b) * 32 + 2 * k + z, 8, stride=64), :] for k in KS], axis=0)
        )
    for i, x in enumerate(swap_blocks(parity, 16)):
        vs[i] = x.astype(BF16)
    get_grad.wait()
    tiles = [
        jnp.concatenate([grad[2 * t].astype(F32), grad[2 * t + 1].astype(F32)], axis=1) for t in range(8)
    ]
    for i, x in enumerate(swap_blocks(tiles, 8)):
        gs[i] = x.astype(BF16)

    pl.semaphore_wait(barrier, len(hello))

    send(gs, gtb.at[f], snd_g.at[0], rcv_g.at[0], (s, fx))
    for i in range(1, NF):
        to = (f + i) % NF
        send(vs.at[to], wbuf.at[0, f], snd_v.at[i - 1], rcv_v.at[i - 1], (s, to))
    for i in range(1, 4):
        send(gs, gtb.at[f], snd_g.at[i], rcv_g.at[i], (s, (f + 2 * i) % NF))
    wbuf[0, f] = vs[f]
    gtb[f] = gs[...]

    get_ker.wait()
    send(kall.at[f, core], kall.at[f, core], snd_k.at[0], rcv_k.at[0], (sx, fx))
    arrived(gtb.at[fx], snd_g.at[0], rcv_g.at[0])
    for i in range(1, 4):
        send(gtb.at[fx], gtb.at[fx], snd_g.at[3 + i], rcv_g.at[3 + i], (s, (f + 2 * i) % NF))

    for i in range(1, NF):
        arrived(wbuf.at[0, (f + NF - i) % NF], snd_v.at[i - 1], rcv_v.at[i - 1])
    send(wbuf.at[0], wbuf.at[1], snd_m.at[0], rcv_m.at[0], (up, f))
    for i, x in enumerate(four_shifts(wbuf[0])):
        rhs[:, i * 128 : i * 128 + 128] = x
    for i in range(1, 4):
        arrived(gtb.at[(f + NF - 2 * i) % NF], snd_g.at[i], rcv_g.at[i])
    for i in range(1, 4):
        arrived(gtb.at[(fx + NF - 2 * i) % NF], snd_g.at[3 + i], rcv_g.at[3 + i])
    arrived(kall.at[fx, core], snd_k.at[0], rcv_k.at[0])
    for n, by in enumerate((2, 6)):
        to = (s, (f + by) % NF)
        send(kall.at[f, core], kall.at[f, core], snd_k.at[1 + n], rcv_k.at[1 + n], to)
        send(kall.at[fx, core], kall.at[fx, core], snd_k.at[3 + n], rcv_k.at[3 + n], to)
    gall = jnp.concatenate([gtb[:, t].reshape(256, 128) for t in range(8)], axis=1)
    own = jnp.dot(gall, rhs[...], preferred_element_type=F32)
    o = [own[:, i * 128 : i * 128 + 128] for i in range(4)]
    shape = (256, 128)
    rt[0] = o[0]
    rt[3] = jnp.where(lane_blocks(shape, (0, 4)), pltpu.roll(o[3], 16, 1), o[2])
    send(rt.at[3 * (1 - core)], s1.at[0], snd_m.at[3], rcv_m.at[3], (sib, f))
    send(vol.at[1], halo_b, snd_h.at[0], rcv_h.at[0], (up, f))
    send(vol.at[:, 15], halo_r, snd_h.at[1], rcv_h.at[1], (s, fup))
    send(vol.at[1, 15], halo_c, snd_h.at[2], rcv_h.at[2], (up, fup))
    send(gtb.at[:, f], gnext.at[0], snd_m.at[1], rcv_m.at[1], (down, f))
    send(gtb.at[:, fup], gnext.at[1], snd_m.at[2], rcv_m.at[2], (down, f))

    arrived(wbuf.at[1], snd_m.at[0], rcv_m.at[0])
    for i, x in enumerate(four_shifts(wbuf[1])):
        rhs[:, i * 128 : i * 128 + 128] = jnp.where(s > 0, x, jnp.zeros_like(x))
    below = jnp.dot(gall, rhs[...], preferred_element_type=F32)
    b = [below[:, i * 128 : i * 128 + 128] for i in range(4)]
    x = jnp.where(lane_blocks(shape, (4, 6)), pltpu.roll(b[1], 112, 1), o[1])
    rt[1] = jnp.where(lane_blocks(shape, (0,)), pltpu.roll(b[3], 16, 1), x)
    rt[2] = jnp.where(lane_blocks(shape, (0, 1)), pltpu.roll(b[2], 32, 1), b[0])
    send(rt.at[2 - core], s1.at[1], snd_m.at[4], rcv_m.at[4], (sib, f))

    for l in range(2):
        arrived(s1.at[l], snd_m.at[3 + l], rcv_m.at[3 + l])
        kept = 3 * core if l == 0 else 1 + core
        asum[l] = (rt[kept] + s1[l]).reshape(16, 16, 128)
        for i in FAR:
            qd = (q + i) % NQ
            n = 15 * l + i - 1
            send(asum.at[l, qd], s2.at[l, i - 1], snd_2.at[n], rcv_2.at[n], (2 * qd + core, f))

    arrived(kall.at[(f + 6) % NF, core], snd_k.at[1], rcv_k.at[1])
    send(kall.at[(f + 6) % NF, core], kall.at[(f + 6) % NF, core], snd_k.at[5], rcv_k.at[5], (s, (f + 2) % NF))
    arrived(kall.at[(fx + 2) % NF, core], snd_k.at[4], rcv_k.at[4])
    send(kall.at[(fx + 2) % NF, core], kall.at[(fx + 2) % NF, core], snd_k.at[6], rcv_k.at[6], (s, (f + 6) % NF))

    homes = []
    for l in range(2):
        for i in range(1, NQ):
            n = 15 * l + i - 1
            arrived(s2.at[l, i - 1], snd_2.at[n], rcv_2.at[n])
        acc = asum[l, q]
        for i in range(1, NQ):
            acc = acc + s2[l, i - 1]
        own3[l] = acc
        kept = 3 * core if l == 0 else 1 + core
        slot = kb.at[f, kept, half]
        got = rcv_3.at[16 * l + 8 * half + f]
        for i in FAR:
            qd = (q + i) % NQ
            send(own3.at[l], slot, snd_3.at[16 * l + i], got, (2 * qd + core, dest))
        homes.append(copy(own3.at[l], slot, snd_3.at[16 * l], got, (s, dest)))

        @pl.when(f != dest)
        def _():
            homes[l].start()

        @pl.when(f == dest)
        def _():
            kb[f, kept, half] = own3[l]

    arrived(kall.at[(f + 2) % NF, core], snd_k.at[2], rcv_k.at[2])
    arrived(kall.at[(fx + 6) % NF, core], snd_k.at[3], rcv_k.at[3])
    arrived(kall.at[(f + 4) % NF, core], snd_k.at[5], rcv_k.at[5])
    arrived(kall.at[(fx + 4) % NF, core], snd_k.at[6], rcv_k.at[6])
    send(kall.at[:, core], kall.at[:, core], snd_m.at[5], rcv_m.at[5], (sib, f))

    arrived(halo_b, snd_h.at[0], rcv_h.at[0])
    arrived(halo_r, snd_h.at[1], rcv_h.at[1])
    arrived(halo_c, snd_h.at[2], rcv_h.at[2])
    low = halo_b[...].astype(F32).reshape(512, 128)
    vf[pl.ds(32, 512), :] = jnp.where(s > 0, low, jnp.zeros_like(low))
    edge = halo_c[...].astype(F32)
    vf[pl.ds(0, 32), :] = jnp.where((s > 0) & (f > 0), edge, jnp.zeros_like(edge))
    for px in range(2):
        edge = halo_r[px].astype(F32)
        vf[pl.ds((1 + px) * 17 * 32, 32), :] = jnp.where(f > 0, edge, jnp.zeros_like(edge))
    for a in range(3):
        for b3 in range(3):
            def cells(z):
                return vf[pl.ds((a * 17 + b3) * 32 + z, 8, stride=64), :]
            for c in range(3):
                col = ((a * 3 + b3) * 3 + c) * 128
                rows = [
                    jnp.zeros((8, 128), F32) if 2 * k + c == 0 else cells(2 * k + c - 1) for k in KS
                ]
                pb[:, col : col + 128] = jnp.concatenate(rows, axis=0).astype(BF16)

    def tap(n):
        return kall[:, :, n].reshape(256, 128)

    arrived(kall.at[:, 1 - core], snd_m.at[5], rcv_m.at[5])
    total = jnp.zeros((256, 128), F32)
    for a in range(3):
        taps = jnp.concatenate([tap(9 * a + n) for n in range(9)], axis=1)
        total = total + dot_t(taps, pb[:, 1152 * a : 1152 * a + 1152])
    fs[...] = total.astype(BF16).reshape(8, 32, 128)
    for i in range(1, NF):
        to = (f + i) % NF
        send(fs.at[to], fb.at[f], snd_f.at[i - 1], rcv_f.at[i - 1], (s, to))
    fb[f] = fs[f]

    arrived(gnext.at[0], snd_m.at[1], rcv_m.at[1])
    arrived(gnext.at[1], snd_m.at[2], rcv_m.at[2])
    picks = jnp.concatenate([selection(dj, dk) for dj in range(2) for dk in range(2)], axis=0)
    here = gtb[:, f].reshape(256, 128)
    nxt = gtb[:, fup].reshape(256, 128)
    nxt = jnp.where(f < NF - 1, nxt, jnp.zeros_like(nxt))
    gv[0] = dot_t(picks, jnp.concatenate([here, nxt], axis=1)).astype(BF16)
    here = gnext[0].reshape(256, 128)
    here = jnp.where(s < NS - 1, here, jnp.zeros_like(here))
    nxt = gnext[1].reshape(256, 128)
    nxt = jnp.where((s < NS - 1) & (f < NF - 1), nxt, jnp.zeros_like(nxt))
    gv[1] = dot_t(picks, jnp.concatenate([here, nxt], axis=1)).astype(BF16)
    steps = (((1, 0),), ((0, 1), (2, 0)))
    for px in range(2):
        for py in range(2):
            for pz in range(2):
                left, right = [], []
                for a, di in steps[px]:
                    for b3, dj in steps[py]:
                        for c, dk in steps[pz]:
                            v = (2 * dj + dk) * 128
                            left.append(gv[di, v : v + 128])
                            right.append(tap(9 * a + 3 * b3 + c))
                res = jnp.dot(
                    jnp.concatenate(left, axis=1), jnp.concatenate(right, axis=0), preferred_element_type=F32
                )
                for n, k in enumerate(KS):
                    igf[pl.ds((px * 16 + py) * 32 + 2 * k + pz, 8, stride=64), :] = res[8 * n : 8 * n + 8]
    ig_out[...] = igf[: 2 * 16 * 32].reshape(2, 16, 32, 128).astype(BF16)

    for l in range(2):
        kept = 3 * core if l == 0 else 1 + core
        for r in range(2):
            for i in range(NF):
                src = (f + i) % NF
                got = copy(
                    own3.at[l], kb.at[src, kept, r], snd_3.at[0], rcv_3.at[16 * l + 8 * r + src], (sib, f)
                )
                if i == 0:
                    @pl.when(2 * f + r != q)
                    def _():
                        got.wait_recv()
                else:
                    got.wait_recv()
        send(kb.at[:, kept], kb.at[:, kept], snd_m.at[6 + l], rcv_m.at[6 + l], (sib, f))

    for i in range(1, NF):
        arrived(fb.at[(f + NF - i) % NF], snd_f.at[i - 1], rcv_f.at[i - 1])
    for t, x in enumerate(swap_blocks([fb[i].astype(F32) for i in range(8)], 8)):
        feat_out[2 * t] = x[:, :64].astype(BF16)
        feat_out[2 * t + 1] = x[:, 64:].astype(BF16)

    factor = float(32 * 64 * 16) ** -0.5
    for l in range(2):
        arrived(kb.at[:, 3 * (1 - core) if l == 0 else 2 - core], snd_m.at[6 + l], rcv_m.at[6 + l])
        for lt in ((0, 3), (1, 2))[l]:
            blocks = swap_blocks([kb[i, lt].reshape(32, 128) for i in range(8)], 16)
            for pos in range(8):
                if (lt, pos) in TAPS:
                    a, b3, c = TAPS[(lt, pos)]
                    kg_out[9 * a + 3 * b3 + c] = blocks[pos] * factor

    for c in sent:
        c.wait_send()
    for c in homes:
        @pl.when(f != dest)
        def _():
            c.wait_send()


def on_device(volume, kernel, out_grad):
    vmem = pl.BlockSpec(memory_space=pltpu.VMEM)
    hbm = pl.BlockSpec(memory_space=pltpu.HBM)
    dma = pltpu.SemaphoreType.DMA
    inputs = (volume, kernel.reshape(27, 2, 16, 128), out_grad.transpose(0, 2, 3, 1).reshape(16, 32, 64))
    feat, ig, kg = pl.pallas_call(
        body,
        out_shape=(
            jax.ShapeDtypeStruct((16, 32, 64), BF16),
            jax.ShapeDtypeStruct((2, 16, 32, 128), BF16),
            jax.ShapeDtypeStruct((27, 32, 128), F32),
        ),
        in_specs=[hbm] * 3,
        out_specs=(vmem,) * 3,
        scratch_shapes=[
            pltpu.VMEM((2, 16, 32, 128), BF16),
            pltpu.VMEM((16, 32, 64), BF16),
            pltpu.VMEM((3 * 17 * 32 + 64, 128), F32),
            pltpu.VMEM((16, 32, 128), BF16),
            pltpu.VMEM((2, 32, 128), BF16),
            pltpu.VMEM((32, 128), BF16),
            pltpu.VMEM((8, 128, 128), BF16),
            pltpu.VMEM((2, 8, 128, 128), BF16),
            pltpu.VMEM((8, 32, 128), BF16),
            pltpu.VMEM((8, 8, 32, 128), BF16),
            pltpu.VMEM((2, 8, 32, 128), BF16),
            pltpu.VMEM((8, 2, 27, 16, 128), BF16),
            pltpu.VMEM((1024, 512), BF16),
            pltpu.VMEM((4, 256, 128), F32),
            pltpu.VMEM((2, 256, 128), F32),
            pltpu.VMEM((2, 16, 16, 128), F32),
            pltpu.VMEM((2, 15, 16, 128), F32),
            pltpu.VMEM((2, 16, 128), F32),
            pltpu.VMEM((8, 4, 2, 16, 128), F32),
            pltpu.VMEM((8, 32, 128), BF16),
            pltpu.VMEM((8, 32, 128), BF16),
            pltpu.VMEM((128, 27 * 128), BF16),
            pltpu.VMEM((2, 512, 256), BF16),
            pltpu.VMEM((2 * 16 * 32 + 64, 128), F32),
            dma((3,)),
            dma((7,)), dma((7,)), dma((7,)), dma((7,)), dma((7,)), dma((7,)),
            dma((3,)), dma((3,)), dma((8,)), dma((8,)), dma((30,)), dma((30,)),
            dma((32,)), dma((32,)), dma((7,)), dma((7,)),
        ],
        compiler_params=pltpu.CompilerParams(
            collective_id=0, has_side_effects=True, vmem_limit_bytes=40 * 1024 * 1024
        ),
        name="conv_fwd_bwd",
    )(*[pltpu.with_memory_space_constraint(x, pltpu.HBM) for x in inputs])
    features = feat.reshape(1, 16, 32, 64).transpose(0, 3, 1, 2)
    return features, ig, kg.reshape(3, 3, 3, 32, 128)


def solution(mesh):
    return jax.shard_map(
        on_device,
        mesh=mesh,
        in_specs=(
            P("space", "filt", None, None),
            P(None, None, None, "filt", None),
            P("space", None, None, "filt"),
        ),
        out_specs=(
            P("space", None, None, "filt"),
            P("space", "filt", None, None),
            P(None, None, None, "filt", None),
        ),
        check_vma=False,
    )
```
